32 devices in a mesh: grp: 8 (over z, y), tm: 4 (over x, core).
Axes of the slice: x: 2, y: 2, z: 4, core: 2. Of those that a mesh axis runs over, the one named last changes fastest.
Arguments:
- samples: float32 [2, 512, 32768], P(None, 'grp', 'tm'), may hold values from -6 to 6
- taps: float32 [4, 1024], replicated, may hold values from -3 to 3
Outputs:
- vis_real: float32 [1024, 512, 512], P(('grp', 'tm'))
- vis_imag: float32 [1024, 512, 512], P(('grp', 'tm'))
The draws below stay inside these ranges and needn't reach their ends.
All inputs are finite; a program needn't handle non-finite values.
Results may differ from the reference program's by a relative error of at most 0.000098.
Values sent between devices are 32-bit elements; how exact they have to be, the bound alone decides.
A program may use at most 192 MiB of HBM per device.

```python
import math
import jax
import jax.numpy as jnp
from jax import lax

C = 1024
INPUTS = 512
TAPS = 4
SPECTRA = 32


def steps_of(stream_key, shape, shards, low, largest):
    gain = 1.0
    for dim, blocks in shards:
        draws = jax.random.uniform(jax.random.fold_in(jax.random.fold_in(stream_key, 6), dim), (blocks,), jnp.float32, low / len(shards), largest / len(shards))
        gain = gain * jnp.repeat(jnp.exp(draws), shape[dim] // blocks).reshape((-1,) + (1,) * (len(shape) - 1 - dim))
    return gain


def bell_draw(own_key, extent, scale, bound, split=(), kind=jnp.bfloat16):
    drawn = scale * jax.random.normal(own_key, extent, jnp.float32)
    if split:
        drawn = drawn * steps_of(own_key, extent, split, -0.22, 0.18)
    return jnp.clip(drawn, -bound, bound).astype(kind)


def setup_inputs(seed: int = 0) -> dict:
    key_list = jax.random.split(jax.random.key(seed), 3)
    return {
        "samples": bell_draw(key_list[0], (2, INPUTS, SPECTRA * C), 1.0, 6.0, ((1, 8), (2, 4)), jnp.float32),
        "taps": bell_draw(key_list[1], (TAPS, C), 0.5, 3.0, (), jnp.float32),
    }


def dft_table(order, channels):
    index = jnp.arange(channels, dtype=jnp.int32)
    phase = (order[:, None] * index[None, :] % channels).astype(jnp.float32) * (2.0 * math.pi / channels)
    factor = 1.0 / math.sqrt(channels)
    cosine = jnp.cos(phase) * factor
    sine = jnp.sin(phase) * factor
    upper = jnp.concatenate([cosine, sine], axis=1)
    lower = jnp.concatenate([-sine, cosine], axis=1)
    return jnp.concatenate([upper, lower], axis=0)

def polyphase(blocks, history, taps):
    extended = jnp.concatenate([history, blocks], axis=2)
    frames = blocks.shape[2]
    filtered = jnp.zeros(blocks.shape, jnp.float32)
    for tap in range(taps.shape[0]):
        filtered = filtered + taps[tap][None, None, None, :] * extended[:, :, tap:tap + frames, :]
    return filtered

def transform(table, filtered):
    channels = filtered.shape[3]
    product = lax.dot_general(table.reshape(2 * channels, 2, channels), filtered, (((1, 2), (0, 3)), ((), ())), precision=lax.Precision.HIGHEST)
    return product.reshape(2, channels, filtered.shape[1], filtered.shape[2])

def gram(spectra, total):
    rotated = jnp.stack([spectra[1], -spectra[0]])
    real_part = jnp.einsum('pcis,pcjs->cij', spectra, spectra, precision=lax.Precision.HIGHEST)
    imag_part = jnp.einsum('pcis,pcjs->cij', rotated, spectra, precision=lax.Precision.HIGHEST)
    return (real_part * (1.0 / total), imag_part * (1.0 / total))

def reference(samples, taps):
    blocks = samples.reshape(2, INPUTS, SPECTRA, C)
    history = jnp.zeros((2, INPUTS, TAPS - 1, C), jnp.float32)
    filtered = polyphase(blocks, history, taps)
    table = dft_table(jnp.arange(C, dtype=jnp.int32), C)
    spectra = transform(table, filtered)
    vis_real, vis_imag = gram(spectra, SPECTRA)
    return (vis_real, vis_imag)
```

```python
import math

import numpy as np
import jax
import jax.numpy as jnp
from jax import lax
from jax.experimental import pallas as pl
from jax.experimental.pallas import tpu as pltpu
from jax.sharding import PartitionSpec as P

RADIX = 8
LANES = 128
ROWS = 8
MIB = 1 << 20
LATER = (4, 2, 2)


def passed_along(value, axis, steps):
    count = lax.axis_size(axis)
    leading, last = (max(0, -steps), min(count, count - steps))
    return lax.ppermute(value, axis, [(source, source + steps) for source in range(leading, last)])


def dft_table(order, channels):
    index = jnp.arange(channels, dtype=jnp.int32)
    phase = (order[:, None] * index[None, :] % channels).astype(jnp.float32) * (
        2.0 * math.pi / channels
    )
    factor = 1.0 / math.sqrt(channels)
    cosine = jnp.cos(phase) * factor
    sine = jnp.sin(phase) * factor
    upper = jnp.concatenate([cosine, sine], axis=1)
    lower = jnp.concatenate([-sine, cosine], axis=1)
    return jnp.concatenate([upper, lower], axis=0)


def polyphase(blocks, history, taps):
    extended = jnp.concatenate([history, blocks], axis=2)
    frames = blocks.shape[2]
    filtered = jnp.zeros(blocks.shape, jnp.float32)
    for tap in range(taps.shape[0]):
        filtered = filtered + taps[tap][None, None, None, :] * extended[:, :, tap : tap + frames, :]
    return filtered


def transform(table, filtered):
    channels = filtered.shape[3]
    product = lax.dot_general(
        table.reshape(2 * channels, 2, channels),
        filtered,
        (((1, 2), (0, 3)), ((), ())),
        precision=lax.Precision.HIGHEST,
    )
    return product.reshape(2, channels, filtered.shape[1], filtered.shape[2])


def pair_products(left, right):
    rotated = jnp.stack([left[1], -left[0]])
    real_part = jnp.einsum("pcis,pcjs->cij", left, right, precision=lax.Precision.HIGHEST)
    imag_part = jnp.einsum("pcis,pcjs->cij", rotated, right, precision=lax.Precision.HIGHEST)
    return (real_part, imag_part)


def general_form(samples, taps):
    channels = taps.shape[1]
    tap_count = taps.shape[0]
    inputs_dev = samples.shape[1]
    blocks = samples.reshape(2, inputs_dev, -1, channels)
    frames = blocks.shape[2]
    last_frames = blocks[:, :, frames - (tap_count - 1) :, :]
    history = passed_along(last_frames, "tm", 1)
    filtered = polyphase(blocks, history, taps)
    position = jnp.arange(channels, dtype=jnp.int32)
    spectra = transform(dft_table(position, channels), filtered)
    turned = lax.all_to_all(
        lax.all_to_all(spectra, "grp", split_axis=1, concat_axis=2, tiled=True),
        "tm",
        split_axis=1,
        concat_axis=3,
        tiled=True,
    )
    total = turned.shape[3]
    real_part, imag_part = pair_products(turned, turned)
    return (real_part * (1.0 / total), imag_part * (1.0 / total))


def radix8(values):
    def add(a, b):
        return (a[0] + b[0], a[1] + b[1])

    def sub(a, b):
        return (a[0] - b[0], a[1] - b[1])

    def minus_i(a):
        return (a[1], -a[0])

    def four(x0, x1, x2, x3):
        s, d = add(x0, x2), sub(x0, x2)
        t, e = add(x1, x3), minus_i(sub(x1, x3))
        return add(s, t), add(d, e), sub(s, t), sub(d, e)

    even = four(values[0], values[2], values[4], values[6])
    odd = list(four(values[1], values[3], values[5], values[7]))
    half = math.sqrt(0.5)
    odd[1] = ((odd[1][0] + odd[1][1]) * half, (odd[1][1] - odd[1][0]) * half)
    odd[2] = minus_i(odd[2])
    odd[3] = ((odd[3][1] - odd[3][0]) * half, -(odd[3][0] + odd[3][1]) * half)
    return [add(a, b) for a, b in zip(even, odd)] + [sub(a, b) for a, b in zip(even, odd)]


def fused_kernel(groups, times, samples_ref, taps_ref, table_ref, twiddle_ref, got_ref, *refs):
    relayed = refs[: len(LATER)]
    front, early, late, mixed, local_sem, halo_sem, send_sem, recv_sem, relay_sem = refs[len(LATER) :]
    tap_count, channels = taps_ref.shape
    inputs_dev = samples_ref.shape[1]
    frames = samples_ref.shape[2] // channels
    half, back = frames // 2, tap_count - 1
    devices = groups * times
    near = devices // 2
    share = early.shape[0] // devices
    direct = share - sum(ref.shape[2] for ref in relayed)
    g, t_own = lax.axis_index("grp"), lax.axis_index("tm")
    me = g * times + t_own
    barrier = pltpu.get_barrier_semaphore()

    def place(other):
        return {"grp": other // times, "tm": other % times}

    def paired(step):
        return sum(
            ((me // (1 << b) + step // (1 << b)) % 2) * (1 << b)
            for b in range(devices.bit_length() - 1)
        )

    @pl.loop(1, devices)
    def _(step):
        pl.semaphore_signal(
            barrier,
            inc=1,
            device_id=place(lax.rem(me + step, devices)),
            device_id_type=pl.DeviceIdType.MESH,
        )

    opening = pltpu.make_async_copy(
        samples_ref.at[:, :, pl.ds(0, half * channels)],
        front.at[:, :, pl.ds(back * channels, half * channels)],
        local_sem.at[0],
    )
    opening.start()
    pl.semaphore_wait(barrier, devices - 1)

    halo = pltpu.make_async_remote_copy(
        src_ref=samples_ref.at[:, :, pl.ds((frames - back) * channels, back * channels)],
        dst_ref=front.at[:, :, pl.ds(0, back * channels)],
        send_sem=halo_sem.at[0],
        recv_sem=halo_sem.at[1],
        device_id={"grp": g, "tm": lax.rem(t_own + 1, times)},
        device_id_type=pl.DeviceIdType.MESH,
    )

    @pl.when(t_own < times - 1)
    def _():
        halo.start()

    def spectra(source, first, target):
        @pl.loop(0, half * (inputs_dev // ROWS))
        def _(work):
            s = work // (inputs_dev // ROWS)
            r = work % (inputs_dev // ROWS)
            rows = pl.ds(pl.multiple_of(r * ROWS, ROWS), ROWS)
            put = pl.ds(pl.multiple_of(work * ROWS, ROWS), ROWS)
            values = []
            for n1 in range(RADIX):
                both = []
                for p in range(2):
                    acc = None
                    for t in range(tap_count):
                        tap = taps_ref[t : t + 1, n1 * LANES : (n1 + 1) * LANES]
                        start = (s + first - back + t) * channels + n1 * LANES
                        term = tap * source[p, rows, pl.ds(pl.multiple_of(start, LANES), LANES)]
                        acc = term if acc is None else acc + term
                    both.append(acc)
                values.append(tuple(both))
            for k1, (re, im) in enumerate(radix8(values)):
                if k1:
                    c = twiddle_ref[0, k1 : k1 + 1, :]
                    d = twiddle_ref[1, k1 : k1 + 1, :]
                    re, im = re * c + im * d, im * c - re * d
                mixed[k1, put, 0:LANES] = re
                mixed[k1, put, LANES : 2 * LANES] = im

        per_half = ROWS // 2
        for k1 in range(RADIX):
            product = lax.dot_general(
                table_ref[...],
                mixed[k1],
                (((1,), (1,)), ((), ())),
                precision=lax.Precision.HIGHEST,
                preferred_element_type=jnp.float32,
            )
            for p in range(2):
                for pair in range(per_half // 2):
                    start = k1 * per_half + p * (per_half // 2) + pair
                    target[pl.ds(start, LANES, stride=RADIX * per_half), :] = product[
                        p * LANES : (p + 1) * LANES, pair * LANES : (pair + 1) * LANES
                    ]

    def rows_of(source, device, first, count):
        return source.at[pl.ds(pl.multiple_of(device * share + first, ROWS), count)]

    def far_copy(phase, source, step):
        other = paired(near + step)
        return pltpu.make_async_remote_copy(
            src_ref=rows_of(source, other, 0, direct),
            dst_ref=got_ref.at[phase, me, pl.ds(0, direct)],
            send_sem=send_sem.at[phase, near + step],
            recv_sem=recv_sem.at[phase, near + step],
            device_id=place(other),
            device_id_type=pl.DeviceIdType.MESH,
        )

    def near_copy(phase, source, step):
        other = paired(step)
        return pltpu.make_async_remote_copy(
            src_ref=rows_of(source, other, 0, share),
            dst_ref=got_ref.at[phase, me],
            send_sem=send_sem.at[phase, step],
            recv_sem=recv_sem.at[phase, step],
            device_id=place(other),
            device_id_type=pl.DeviceIdType.MESH,
        )

    def relay_parts():
        first = direct
        for part, ref in enumerate(relayed):
            yield part, ref, first, ref.shape[2]
            first += ref.shape[2]

    def relay_copy(phase, source, step, part, ref, first, count):
        return pltpu.make_async_remote_copy(
            src_ref=rows_of(source, paired(near + step), first, count),
            dst_ref=ref.at[phase, lax.rem(me, near)],
            send_sem=relay_sem.at[0, phase, part, step],
            recv_sem=relay_sem.at[1, phase, part, step],
            device_id=place(paired(step)),
            device_id_type=pl.DeviceIdType.MESH,
        )

    def kept(phase, source):
        yield pltpu.make_async_copy(
            rows_of(source, me, 0, share), got_ref.at[phase, me], local_sem.at[1 + phase]
        )
        for part, ref, first, count in relay_parts():
            yield pltpu.make_async_copy(
                rows_of(source, paired(near), first, count),
                ref.at[phase, lax.rem(me, near)],
                relay_sem.at[0, phase, part, 0],
            )

    def send(phase, source):
        @pl.loop(0, near)
        def _(step):
            far_copy(phase, source, step).start()

            @pl.when(step > 0)
            def _():
                near_copy(phase, source, step).start()
                for args in relay_parts():
                    relay_copy(phase, source, step, *args).start()

        for copy in kept(phase, source):
            copy.start()

    spectra(samples_ref, half, early)
    send(0, early)

    @pl.when(t_own == 0)
    def _():
        front[:, :, 0 : back * channels] = jnp.zeros(
            (2, inputs_dev, back * channels), jnp.float32
        )

    @pl.when(t_own > 0)
    def _():
        halo.wait_recv()

    @pl.when(t_own < times - 1)
    def _():
        halo.wait_send()

    opening.wait()
    spectra(front, back, late)
    send(1, late)

    for phase, source in enumerate((early, late)):
        for copy in kept(phase, source):
            copy.wait()

        @pl.loop(0, near)
        def _(step, phase=phase, source=source):
            far_copy(phase, source, step).wait()

            @pl.when(step > 0)
            def _():
                near_copy(phase, source, step).wait()
                for args in relay_parts():
                    relay_copy(phase, source, step, *args).wait()


def tables(channels):
    n2 = np.arange(LANES)
    phase = 2.0 * np.pi * np.outer(n2, n2) / LANES
    c, s = np.cos(phase), np.sin(phase)
    table = np.block([[c, s], [-s, c]]) / math.sqrt(channels)
    turn = 2.0 * np.pi * np.outer(np.arange(RADIX), n2) / channels
    twiddle = np.stack([np.cos(turn), np.sin(turn)])
    return jnp.asarray(table, jnp.float32), jnp.asarray(twiddle, jnp.float32)


def make_spectra(samples, taps, groups, times):
    tap_count, channels = taps.shape
    inputs_dev = samples.shape[1]
    half = samples.shape[2] // channels // 2
    devices = groups * times
    table, twiddle = tables(channels)
    rows = channels * ROWS // 2

    def body(*refs):
        fused_kernel(groups, times, *refs)

    return pl.pallas_call(
        body,
        out_shape=[jax.ShapeDtypeStruct((2, devices, rows // devices, LANES), jnp.float32)]
        + [
            jax.ShapeDtypeStruct((2, devices // 2, count * ROWS // 2, LANES), jnp.float32)
            for count in LATER
        ],
        in_specs=[pl.BlockSpec(memory_space=pltpu.VMEM)] * 4,
        out_specs=[pl.BlockSpec(memory_space=pltpu.VMEM)] * (1 + len(LATER)),
        scratch_shapes=[
            pltpu.VMEM((2, inputs_dev, (half + tap_count - 1) * channels), jnp.float32),
            pltpu.VMEM((rows, LANES), jnp.float32),
            pltpu.VMEM((rows, LANES), jnp.float32),
            pltpu.VMEM((RADIX, half * inputs_dev, 2 * LANES), jnp.float32),
            pltpu.SemaphoreType.DMA((3,)),
            pltpu.SemaphoreType.DMA((2,)),
            pltpu.SemaphoreType.DMA((2, devices)),
            pltpu.SemaphoreType.DMA((2, devices)),
            pltpu.SemaphoreType.DMA((2, 2, len(LATER), devices // 2)),
        ],
        compiler_params=pltpu.CompilerParams(
            collective_id=0, has_side_effects=True, vmem_limit_bytes=40 * MIB
        ),
    )(samples, taps, table, twiddle)


def gram_kernel(groups, times, total, relayed, got_ref, *refs):
    real_ref, imag_ref = refs[-2:]
    near = groups * times // 2
    in_first = lax.axis_index("grp") < groups // 2 if relayed else None
    lane = lax.broadcasted_iota(jnp.int32, (ROWS, LANES), 1)
    row = lax.broadcasted_iota(jnp.int32, (ROWS, LANES), 0)
    low, upper = lane < LANES // 2, row < ROWS // 2
    first = row % (ROWS // 2) < ROWS // 4

    def split(values):
        high = values.astype(jnp.bfloat16)
        return high, (values - high.astype(jnp.float32)).astype(jnp.bfloat16)

    def stacked(values):
        high, low_part = split(values)
        return jnp.concatenate([high, low_part, low_part, high], axis=0)

    @pl.loop(0, got_ref.shape[2])
    def _(pair):
        for parity in range(2):
            def tile(source):
                a, b = got_ref[0, source, pair], got_ref[1, source, pair]
                if relayed:
                    is_near = in_first if source < near else jnp.logical_not(in_first)
                    a = jnp.where(is_near, a, refs[0][0, source % near, pair])
                    b = jnp.where(is_near, b, refs[0][1, source % near, pair])
                if parity == 0:
                    return jnp.where(upper, a, pltpu.roll(b, ROWS // 2, 0))
                return jnp.where(upper, pltpu.roll(a, ROWS // 2, 0), b)

            plain, turned = [], []
            for t in range(times):
                parts = ([], [])
                for m in range(groups // 2):
                    x, y = tile(2 * m * times + t), tile((2 * m + 1) * times + t)
                    parts[0].append(jnp.where(low, x, pltpu.roll(y, LANES // 2, 1)))
                    parts[1].append(jnp.where(low, pltpu.roll(x, LANES // 2, 1), y))
                for tiles in parts:
                    plain.append(jnp.concatenate(tiles, axis=1))
                    turned.append(
                        jnp.concatenate(
                            [
                                jnp.where(
                                    first,
                                    -pltpu.roll(v, ROWS - ROWS // 4, 0),
                                    pltpu.roll(v, ROWS // 4, 0),
                                )
                                for v in tiles
                            ],
                            axis=1,
                        )
                    )

            whole = jnp.concatenate(plain, axis=0)
            high, low_part = split(whole * (1.0 / total))
            left = jnp.concatenate(
                [high.astype(jnp.float32), low_part.astype(jnp.float32)], axis=0
            ).T.astype(jnp.bfloat16)
            left = jnp.concatenate([left, left], axis=1)
            c = 2 * pair + parity
            real_ref[c] = jnp.dot(left, stacked(whole), preferred_element_type=jnp.float32)
            imag_ref[c] = jnp.dot(
                left,
                stacked(jnp.concatenate(turned, axis=0)),
                preferred_element_type=jnp.float32,
            )


def gram(got, groups, times, total, inputs, start, count, arrived=None, so_far=()):
    devices, own_channels = got.shape[1], 2 * got.shape[2]
    step = 2
    relayed = arrived is not None

    def body(*refs):
        gram_kernel(groups, times, total, relayed, *refs)

    shape = jax.ShapeDtypeStruct((own_channels, inputs, inputs), jnp.float32)
    block = pl.BlockSpec((step, inputs, inputs), lambda i: (start // step + i, 0, 0))
    tile = (step // 2, ROWS, LANES)
    in_specs = [pl.BlockSpec((2, devices) + tile, lambda i: (0, 0, start // step + i, 0, 0))]
    if relayed:
        in_specs.append(pl.BlockSpec((2, devices // 2) + tile, lambda i: (0, 0, i, 0, 0)))
    first = len(in_specs)
    in_specs += [pl.BlockSpec(memory_space=pl.ANY)] * len(so_far)
    return pl.pallas_call(
        body,
        grid=(count // step,),
        out_shape=(shape, shape),
        in_specs=in_specs,
        out_specs=(block, block),
        input_output_aliases={first + i: i for i in range(len(so_far))},
        cost_estimate=pl.CostEstimate(
            flops=count * 2 * inputs * inputs * 4 * ROWS * times * 4,
            bytes_accessed=count * 2 * inputs * inputs * 4,
            transcendentals=0,
        ),
        compiler_params=pltpu.CompilerParams(vmem_limit_bytes=40 * MIB),
    )(got, *((arrived,) if relayed else ()), *so_far)


def solution(mesh):
    groups, times = mesh.shape["grp"], mesh.shape["tm"]
    devices = groups * times

    def per_device(samples, taps):
        tap_count, channels = taps.shape
        inputs_dev = samples.shape[1]
        frames = samples.shape[2] // channels
        tiled = (
            channels == RADIX * LANES
            and inputs_dev * 2 == LANES
            and frames == ROWS
            and groups % 2 == 0
            and channels % (4 * devices) == 0
            and channels // devices > sum(LATER)
            and devices & (devices - 1) == 0
            and tap_count - 1 <= frames // 2
            and 2 * frames * times * 2 == LANES
        )
        if not tiled:
            return general_form(samples, taps)
        got, *relayed = make_spectra(samples, taps, groups, times)
        own = channels // devices
        across = [(g, (g + groups // 2) % groups) for g in range(groups)]
        arrived = [lax.ppermute(part, "grp", across) for part in relayed]
        got = got.reshape(2, devices, own // 2, ROWS, LANES)
        sizes = (groups, times, frames * times, inputs_dev * groups)
        start = own - sum(LATER)
        so_far = gram(got, *sizes, 0, start)
        for count, part in zip(LATER, arrived):
            part = part.reshape(2, devices // 2, count // 2, ROWS, LANES)
            so_far = gram(got, *sizes, start, count, part, so_far)
            start += count
        return so_far

    return jax.shard_map(
        per_device,
        mesh=mesh,
        in_specs=(P(None, "grp", "tm"), P()),
        out_specs=(P(("grp", "tm"), None, None), P(("grp", "tm"), None, None)),
        check_vma=False,
    )
```

```python
import math

import numpy as np
import jax
import jax.numpy as jnp
from jax import lax
from jax.experimental import pallas as pl
from jax.experimental.pallas import tpu as pltpu
from jax.sharding import PartitionSpec as P

RADIX = 8
LANES = 128
ROWS = 8
MIB = 1 << 20
PARTS = 2
SLOTS = 4
LATER = (4, 4)
AHEAD = (4,)


def passed_along(value, axis, steps):
    count = lax.axis_size(axis)
    leading, last = (max(0, -steps), min(count, count - steps))
    return lax.ppermute(value, axis, [(source, source + steps) for source in range(leading, last)])


def dft_table(order, channels):
    index = jnp.arange(channels, dtype=jnp.int32)
    phase = (order[:, None] * index[None, :] % channels).astype(jnp.float32) * (
        2.0 * math.pi / channels
    )
    factor = 1.0 / math.sqrt(channels)
    cosine = jnp.cos(phase) * factor
    sine = jnp.sin(phase) * factor
    upper = jnp.concatenate([cosine, sine], axis=1)
    lower = jnp.concatenate([-sine, cosine], axis=1)
    return jnp.concatenate([upper, lower], axis=0)


def polyphase(blocks, history, taps):
    extended = jnp.concatenate([history, blocks], axis=2)
    frames = blocks.shape[2]
    filtered = jnp.zeros(blocks.shape, jnp.float32)
    for tap in range(taps.shape[0]):
        filtered = filtered + taps[tap][None, None, None, :] * extended[:, :, tap : tap + frames, :]
    return filtered


def transform(table, filtered):
    channels = filtered.shape[3]
    product = lax.dot_general(
        table.reshape(2 * channels, 2, channels),
        filtered,
        (((1, 2), (0, 3)), ((), ())),
        precision=lax.Precision.HIGHEST,
    )
    return product.reshape(2, channels, filtered.shape[1], filtered.shape[2])


def pair_products(left, right):
    rotated = jnp.stack([left[1], -left[0]])
    real_part = jnp.einsum("pcis,pcjs->cij", left, right, precision=lax.Precision.HIGHEST)
    imag_part = jnp.einsum("pcis,pcjs->cij", rotated, right, precision=lax.Precision.HIGHEST)
    return (real_part, imag_part)


def general_form(samples, taps):
    channels = taps.shape[1]
    tap_count = taps.shape[0]
    inputs_dev = samples.shape[1]
    blocks = samples.reshape(2, inputs_dev, -1, channels)
    frames = blocks.shape[2]
    last_frames = blocks[:, :, frames - (tap_count - 1) :, :]
    history = passed_along(last_frames, "tm", 1)
    filtered = polyphase(blocks, history, taps)
    position = jnp.arange(channels, dtype=jnp.int32)
    spectra = transform(dft_table(position, channels), filtered)
    turned = lax.all_to_all(
        lax.all_to_all(spectra, "grp", split_axis=1, concat_axis=2, tiled=True),
        "tm",
        split_axis=1,
        concat_axis=3,
        tiled=True,
    )
    total = turned.shape[3]
    real_part, imag_part = pair_products(turned, turned)
    return (real_part * (1.0 / total), imag_part * (1.0 / total))


def radix8(values):
    def add(a, b):
        return (a[0] + b[0], a[1] + b[1])

    def sub(a, b):
        return (a[0] - b[0], a[1] - b[1])

    def minus_i(a):
        return (a[1], -a[0])

    def four(x0, x1, x2, x3):
        s, d = add(x0, x2), sub(x0, x2)
        t, e = add(x1, x3), minus_i(sub(x1, x3))
        return add(s, t), add(d, e), sub(s, t), sub(d, e)

    even = four(values[0], values[2], values[4], values[6])
    odd = list(four(values[1], values[3], values[5], values[7]))
    half = math.sqrt(0.5)
    odd[1] = ((odd[1][0] + odd[1][1]) * half, (odd[1][1] - odd[1][0]) * half)
    odd[2] = minus_i(odd[2])
    odd[3] = ((odd[3][1] - odd[3][0]) * half, -(odd[3][0] + odd[3][1]) * half)
    return [add(a, b) for a, b in zip(even, odd)] + [sub(a, b) for a, b in zip(even, odd)]


def split(values):
    high = values.astype(jnp.bfloat16)
    return high, (values - high.astype(jnp.float32)).astype(jnp.bfloat16)


def fused_kernel(
    groups, times, samples_in, taps_in, table_in, twiddle_in, got_ref, *refs
):
    relayed = refs[: len(LATER)]
    (
        frames_ref,
        taps_ref,
        table_ref,
        twiddle_ref,
        early,
        late,
        mixed,
        load_sem,
        halo_sem,
        kept_sem,
        send_sem,
        recv_sem,
        relay_sem,
    ) = refs[len(LATER) :]
    tap_count, channels = taps_ref.shape
    inputs_dev = samples_in.shape[1]
    frames = samples_in.shape[2] // channels
    half, back = frames // 2, tap_count - 1
    devices = groups * times
    near = devices // 2
    rows_part = early.shape[0] // PARTS
    share = rows_part // devices
    later_rows = sum(ref.shape[2] for ref in relayed)
    g, t_own = lax.axis_index("grp"), lax.axis_index("tm")
    me = g * times + t_own
    slot = lax.rem(me, near)
    barrier = pltpu.get_barrier_semaphore()

    def place(other):
        return {"grp": other // times, "tm": other % times}

    def paired(step):
        return sum(
            ((me // (1 << b) + step // (1 << b)) % 2) * (1 << b)
            for b in range(devices.bit_length() - 1)
        )

    @pl.loop(1, devices)
    def _(step):
        pl.semaphore_signal(
            barrier,
            inc=1,
            device_id=place(lax.rem(me + step, devices)),
            device_id_type=pl.DeviceIdType.MESH,
        )

    chunk = 2 * ROWS
    chunks = inputs_dev // chunk

    def load(number):
        rows = pl.ds(pl.multiple_of(number * chunk, chunk), chunk)
        return pltpu.make_async_copy(
            samples_in.at[:, rows],
            frames_ref.at[:, rows, pl.ds(back * channels, frames * channels)],
            load_sem.at[number],
        )

    tables_in = [
        pltpu.make_async_copy(source, target, load_sem.at[chunks + number])
        for number, (source, target) in enumerate(
            ((taps_in, taps_ref), (twiddle_in, twiddle_ref), (table_in, table_ref))
        )
    ]
    tables_in[0].start()
    tables_in[1].start()

    @pl.loop(0, chunks)
    def _(number):
        load(number).start()

    tables_in[2].start()
    tables_in[0].wait()
    tables_in[1].wait()

    halo = pltpu.make_async_remote_copy(
        src_ref=samples_in.at[:, :, pl.ds((frames - back) * channels, back * channels)],
        dst_ref=frames_ref.at[:, :, pl.ds(0, back * channels)],
        send_sem=halo_sem.at[0],
        recv_sem=halo_sem.at[1],
        device_id={"grp": g, "tm": lax.rem(t_own + 1, times)},
        device_id_type=pl.DeviceIdType.MESH,
    )

    def filtered(first, loading):
        pairs = half // 2

        @pl.loop(0, pairs * (inputs_dev // ROWS))
        def _(work):
            s = 2 * (work % pairs)
            r = work // pairs
            if loading:
                steps = pairs * (chunk // ROWS)

                @pl.when(work % steps == 0)
                def _():
                    load(work // steps).wait()

            rows = pl.ds(pl.multiple_of(r * ROWS, ROWS), ROWS)
            values = ([], [])
            for n1 in range(RADIX):
                both = ([], [])
                taps = [
                    taps_ref[t : t + 1, n1 * LANES : (n1 + 1) * LANES] for t in range(tap_count)
                ]
                for p in range(2):
                    read = []
                    for t in range(tap_count + 1):
                        start = (s + first + t) * channels + n1 * LANES
                        read.append(
                            frames_ref[p, rows, pl.ds(pl.multiple_of(start, LANES), LANES)]
                        )
                    for f in range(2):
                        acc = taps[0] * read[f]
                        for t in range(1, tap_count):
                            acc = acc + taps[t] * read[f + t]
                        both[f].append(acc)
                for f in range(2):
                    values[f].append(tuple(both[f]))
            for f in range(2):
                put = pl.ds(pl.multiple_of((s + f) * inputs_dev + r * ROWS, ROWS), ROWS)
                for k1, (re, im) in enumerate(radix8(values[f])):
                    if k1:
                        c = twiddle_ref[0, k1 : k1 + 1, :]
                        d = twiddle_ref[1, k1 : k1 + 1, :]
                        re, im = re * c + im * d, im * c - re * d
                    mixed[k1, put, 0:LANES] = re
                    mixed[k1, put, LANES : 2 * LANES] = im

    per_part = RADIX // PARTS
    per_half = ROWS // 2

    def transformed(part, target):
        for inner in range(per_part):
            high, low = split(mixed[part * per_part + inner])
            product = lax.dot_general(
                table_ref[...],
                jnp.concatenate([high, low, high], axis=1),
                (((1,), (1,)), ((), ())),
                preferred_element_type=jnp.float32,
            )
            for p in range(2):
                for pair in range(per_half // 2):
                    start = part * rows_part + inner * per_half + p * (per_half // 2) + pair
                    target[pl.ds(start, LANES, stride=per_part * per_half), :] = product[
                        p * LANES : (p + 1) * LANES, pair * LANES : (pair + 1) * LANES
                    ]

    def rows_of(source, part, device, first, count):
        start = part * rows_part + device * share + first
        return source.at[pl.ds(pl.multiple_of(start, ROWS), count)]

    def kept_rows(part):
        return share - later_rows if part == PARTS - 1 else share

    def to_rows(phase, part, count):
        return got_ref.at[phase, me, pl.ds(part * share, count)]

    def far_copy(phase, part, source, step):
        other = paired(near + step)
        count = kept_rows(part)
        return pltpu.make_async_remote_copy(
            src_ref=rows_of(source, part, other, 0, count),
            dst_ref=to_rows(phase, part, count),
            send_sem=send_sem.at[phase, part, near + step],
            recv_sem=recv_sem.at[phase, part, near + step],
            device_id=place(other),
            device_id_type=pl.DeviceIdType.MESH,
        )

    def near_copy(phase, part, source, step):
        other = paired(step)
        return pltpu.make_async_remote_copy(
            src_ref=rows_of(source, part, other, 0, share),
            dst_ref=to_rows(phase, part, share),
            send_sem=send_sem.at[phase, part, step],
            recv_sem=recv_sem.at[phase, part, step],
            device_id=place(other),
            device_id_type=pl.DeviceIdType.MESH,
        )

    def pieces(part):
        first = share - later_rows
        for number, ref in enumerate(relayed if part == PARTS - 1 else ()):
            yield number, ref, first, ref.shape[2]
            first += ref.shape[2]

    def relay_copy(phase, part, source, step, number, ref, first, count):
        return pltpu.make_async_remote_copy(
            src_ref=rows_of(source, part, paired(near + step), first, count),
            dst_ref=ref.at[phase, slot],
            send_sem=relay_sem.at[0, phase, number, step],
            recv_sem=relay_sem.at[1, phase, number, step],
            device_id=place(paired(step)),
            device_id_type=pl.DeviceIdType.MESH,
        )

    def kept(phase, part, source):
        yield pltpu.make_async_copy(
            rows_of(source, part, me, 0, share),
            to_rows(phase, part, share),
            kept_sem.at[phase, part],
        )
        for number, ref, first, count in pieces(part):
            yield pltpu.make_async_copy(
                rows_of(source, part, paired(near), first, count),
                ref.at[phase, slot],
                relay_sem.at[0, phase, number, 0],
            )

    def each_copy(phase, part, source, act):
        @pl.loop(0, near)
        def _(step):
            act(far_copy(phase, part, source, step))

            @pl.when(step > 0)
            def _():
                act(near_copy(phase, part, source, step))
                for args in pieces(part):
                    act(relay_copy(phase, part, source, step, *args))

        for copy in kept(phase, part, source):
            act(copy)

    filtered(half, True)
    tables_in[2].wait()
    transformed(0, early)
    pl.semaphore_wait(barrier, devices - 1)

    @pl.when(t_own < times - 1)
    def _():
        halo.start()

    each_copy(0, 0, early, lambda copy: copy.start())
    for part in range(1, PARTS):
        transformed(part, early)
        each_copy(0, part, early, lambda copy: copy.start())

    @pl.when(t_own == 0)
    def _():
        frames_ref[:, :, 0 : back * channels] = jnp.zeros(
            (2, inputs_dev, back * channels), jnp.float32
        )

    @pl.when(t_own > 0)
    def _():
        halo.wait_recv()

    filtered(0, False)
    for part in range(PARTS):
        transformed(part, late)
        each_copy(1, part, late, lambda copy: copy.start())

    @pl.when(t_own < times - 1)
    def _():
        halo.wait_send()

    for phase, source in enumerate((early, late)):
        for part in range(PARTS):
            each_copy(phase, part, source, lambda copy: copy.wait())


def tables(channels):
    n2 = np.arange(LANES)
    phase = 2.0 * np.pi * np.outer(n2, n2) / LANES
    c, s = np.cos(phase), np.sin(phase)
    table = (np.block([[c, s], [-s, c]]) / math.sqrt(channels)).astype(np.float32)
    high = table.astype(jnp.bfloat16)
    low = (table - high.astype(np.float32)).astype(jnp.bfloat16)
    turn = 2.0 * np.pi * np.outer(np.arange(RADIX), n2) / channels
    twiddle = np.stack([np.cos(turn), np.sin(turn)])
    return jnp.asarray(np.concatenate([high, high, low], axis=1)), jnp.asarray(twiddle, jnp.float32)


def make_spectra(samples, taps, groups, times):
    tap_count, channels = taps.shape
    inputs_dev = samples.shape[1]
    frames = samples.shape[2] // channels
    half = frames // 2
    devices = groups * times
    table, twiddle = tables(channels)
    rows = channels * ROWS // 2

    def body(*refs):
        fused_kernel(groups, times, *refs)

    return pl.pallas_call(
        body,
        out_shape=[jax.ShapeDtypeStruct((2, devices, rows // devices, LANES), jnp.float32)]
        + [
            jax.ShapeDtypeStruct((2, devices // 2, count * ROWS // 2, LANES), jnp.float32)
            for count in LATER
        ],
        in_specs=[pl.BlockSpec(memory_space=pltpu.HBM)] * 4,
        out_specs=[pl.BlockSpec(memory_space=pltpu.VMEM)] * (1 + len(LATER)),
        scratch_shapes=[
            pltpu.VMEM((2, inputs_dev, (frames + tap_count - 1) * channels), jnp.float32),
            pltpu.VMEM(taps.shape, jnp.float32),
            pltpu.VMEM(table.shape, jnp.bfloat16),
            pltpu.VMEM(twiddle.shape, jnp.float32),
            pltpu.VMEM((rows, LANES), jnp.float32),
            pltpu.VMEM((rows, LANES), jnp.float32),
            pltpu.VMEM((RADIX, half * inputs_dev, 2 * LANES), jnp.float32),
            pltpu.SemaphoreType.DMA((inputs_dev // (2 * ROWS) + 3,)),
            pltpu.SemaphoreType.DMA((2,)),
            pltpu.SemaphoreType.DMA((2, PARTS)),
            pltpu.SemaphoreType.DMA((2, PARTS, devices)),
            pltpu.SemaphoreType.DMA((2, PARTS, devices)),
            pltpu.SemaphoreType.DMA((2, 2, len(LATER), devices // 2)),
        ],
        compiler_params=pltpu.CompilerParams(
            collective_id=0, has_side_effects=True, vmem_limit_bytes=40 * MIB
        ),
    )(*(pltpu.with_memory_space_constraint(x, pltpu.HBM) for x in (samples, taps, table, twiddle)))


def gram_kernel(groups, times, total, start, count, relayed, got_ref, *refs):
    real_out, imag_out, real_ref, imag_ref, sem = refs[-5:]
    near = groups * times // 2
    own_channels = real_out.shape[0]
    in_first = lax.axis_index("grp") < groups // 2 if relayed else None
    lane = lax.broadcasted_iota(jnp.int32, (ROWS, LANES), 1)
    row = lax.broadcasted_iota(jnp.int32, (ROWS, LANES), 0)
    low, upper = lane < LANES // 2, row < ROWS // 2
    first = row % (ROWS // 2) < ROWS // 4

    def stacked(values):
        high, low_part = split(values)
        return jnp.concatenate([high, low_part, low_part, high], axis=0)

    def channel_of(pair):
        per_block = RADIX // PARTS // 2
        blocks = own_channels // RADIX
        block = pair // per_block
        return (
            (block % blocks) * RADIX + (block // blocks) * (2 * per_block) + 2 * (pair % per_block)
        )

    def writes(turn, channel):
        at = turn % SLOTS
        return [
            pltpu.make_async_copy(ref.at[at], out.at[channel], sem.at[number, at])
            for number, (ref, out) in enumerate(((real_ref, real_out), (imag_ref, imag_out)))
        ]

    @pl.loop(0, count // 2)
    def _(step):
        pair = start // 2 + step
        for parity in range(2):
            def tile(source):
                a, b = got_ref[0, source, pair], got_ref[1, source, pair]
                if relayed:
                    is_near = in_first if source < near else jnp.logical_not(in_first)
                    a = jnp.where(is_near, a, refs[0][0, source % near, step])
                    b = jnp.where(is_near, b, refs[0][1, source % near, step])
                if parity == 0:
                    return jnp.where(upper, a, pltpu.roll(b, ROWS // 2, 0))
                return jnp.where(upper, pltpu.roll(a, ROWS // 2, 0), b)

            plain, turned = [], []
            for t in range(times):
                parts = ([], [])
                for m in range(groups // 2):
                    x, y = tile(2 * m * times + t), tile((2 * m + 1) * times + t)
                    parts[0].append(jnp.where(low, x, pltpu.roll(y, LANES // 2, 1)))
                    parts[1].append(jnp.where(low, pltpu.roll(x, LANES // 2, 1), y))
                for tiles in parts:
                    plain.append(jnp.concatenate(tiles, axis=1))
                    turned.append(
                        jnp.concatenate(
                            [
                                jnp.where(
                                    first,
                                    -pltpu.roll(v, ROWS - ROWS // 4, 0),
                                    pltpu.roll(v, ROWS // 4, 0),
                                )
                                for v in tiles
                            ],
                            axis=1,
                        )
                    )

            whole = jnp.concatenate(plain, axis=0)
            high, low_part = split(whole * (1.0 / total))
            left = jnp.concatenate(
                [high.astype(jnp.float32), low_part.astype(jnp.float32)], axis=0
            ).T.astype(jnp.bfloat16)
            left = jnp.concatenate([left, left], axis=1)
            turn = 2 * step + parity
            at = turn % SLOTS

            @pl.when(turn >= SLOTS)
            def _():
                for write in writes(turn, 0):
                    write.wait()

            real_ref[at] = jnp.dot(left, stacked(whole), preferred_element_type=jnp.float32)
            imag_ref[at] = jnp.dot(
                left,
                stacked(jnp.concatenate(turned, axis=0)),
                preferred_element_type=jnp.float32,
            )
            for write in writes(turn, channel_of(pair) + parity):
                write.start()

    for turn in range(max(0, count - SLOTS), count):
        for write in writes(turn, 0):
            write.wait()


def gram(got, groups, times, total, inputs, start, count, arrived=None, so_far=()):
    own_channels = 2 * got.shape[2]
    relayed = arrived is not None

    def body(*refs):
        gram_kernel(groups, times, total, start, count, relayed, *refs)

    shape = jax.ShapeDtypeStruct((own_channels, inputs, inputs), jnp.float32)
    here = 1 + relayed
    return pl.pallas_call(
        body,
        out_shape=(shape, shape),
        in_specs=[pl.BlockSpec(memory_space=pltpu.VMEM)] * here
        + [pl.BlockSpec(memory_space=pl.ANY)] * len(so_far),
        out_specs=(pl.BlockSpec(memory_space=pltpu.HBM),) * 2,
        input_output_aliases={here + i: i for i in range(len(so_far))},
        scratch_shapes=[
            pltpu.VMEM((SLOTS, inputs, inputs), jnp.float32),
            pltpu.VMEM((SLOTS, inputs, inputs), jnp.float32),
            pltpu.SemaphoreType.DMA((2, SLOTS)),
        ],
        cost_estimate=pl.CostEstimate(
            flops=count * 2 * inputs * inputs * 4 * ROWS * times * 4,
            bytes_accessed=count * 2 * inputs * inputs * 4,
            transcendentals=0,
        ),
        compiler_params=pltpu.CompilerParams(vmem_limit_bytes=24 * MIB),
    )(got, *((arrived,) if relayed else ()), *so_far)


def solution(mesh):
    groups, times = mesh.shape["grp"], mesh.shape["tm"]
    devices = groups * times

    def per_device(samples, taps):
        tap_count, channels = taps.shape
        inputs_dev = samples.shape[1]
        frames = samples.shape[2] // channels
        tiled = (
            channels == RADIX * LANES
            and inputs_dev * 2 == LANES
            and frames == ROWS
            and groups % 2 == 0
            and channels % (RADIX * devices) == 0
            and channels // devices // PARTS > sum(LATER)
            and devices & (devices - 1) == 0
            and tap_count - 1 <= frames // 2
            and 2 * frames * times * 2 == LANES
        )
        if not tiled:
            return general_form(samples, taps)
        got, *relayed = make_spectra(samples, taps, groups, times)
        own = channels // devices
        across = [(g, (g + groups // 2) % groups) for g in range(groups)]
        got = got.reshape(2, devices, own // 2, ROWS, LANES)
        sizes = (groups, times, frames * times, inputs_dev * groups)
        bounds = (0,) + AHEAD + (own - sum(LATER),)
        arrived, so_far = [], ()
        for number, part in enumerate(relayed):
            if number:
                part, so_far = lax.optimization_barrier((part, so_far))
            arrived.append(lax.ppermute(part, "grp", across))
            start, end = bounds[number], bounds[number + 1]
            so_far = gram(got, *sizes, start, end - start, None, so_far)
        start = bounds[-1]
        for count, part in zip(LATER, arrived):
            part = part.reshape(2, devices // 2, count // 2, ROWS, LANES)
            so_far = gram(got, *sizes, start, count, part, so_far)
            start += count
        return so_far

    return jax.shard_map(
        per_device,
        mesh=mesh,
        in_specs=(P(None, "grp", "tm"), P()),
        out_specs=(P(("grp", "tm"), None, None), P(("grp", "tm"), None, None)),
        check_vma=False,
    )
```

```python
import math

import numpy as np
import jax
import jax.numpy as jnp
from jax import lax
from jax.experimental import pallas as pl
from jax.experimental.pallas import tpu as pltpu
from jax.sharding import PartitionSpec as P

RADIX = 8
LANES = 128
ROWS = 8
MIB = 1 << 20
PARTS = 4
SLOTS = 4
LATER = (4, 4)
AHEAD = (4,)


def passed_along(value, axis, steps):
    count = lax.axis_size(axis)
    leading, last = (max(0, -steps), min(count, count - steps))
    return lax.ppermute(value, axis, [(source, source + steps) for source in range(leading, last)])


def dft_table(order, channels):
    index = jnp.arange(channels, dtype=jnp.int32)
    phase = (order[:, None] * index[None, :] % channels).astype(jnp.float32) * (
        2.0 * math.pi / channels
    )
    factor = 1.0 / math.sqrt(channels)
    cosine = jnp.cos(phase) * factor
    sine = jnp.sin(phase) * factor
    upper = jnp.concatenate([cosine, sine], axis=1)
    lower = jnp.concatenate([-sine, cosine], axis=1)
    return jnp.concatenate([upper, lower], axis=0)


def polyphase(blocks, history, taps):
    extended = jnp.concatenate([history, blocks], axis=2)
    frames = blocks.shape[2]
    filtered = jnp.zeros(blocks.shape, jnp.float32)
    for tap in range(taps.shape[0]):
        filtered = filtered + taps[tap][None, None, None, :] * extended[:, :, tap : tap + frames, :]
    return filtered


def transform(table, filtered):
    channels = filtered.shape[3]
    product = lax.dot_general(
        table.reshape(2 * channels, 2, channels),
        filtered,
        (((1, 2), (0, 3)), ((), ())),
        precision=lax.Precision.HIGHEST,
    )
    return product.reshape(2, channels, filtered.shape[1], filtered.shape[2])


def pair_products(left, right):
    rotated = jnp.stack([left[1], -left[0]])
    real_part = jnp.einsum("pcis,pcjs->cij", left, right, precision=lax.Precision.HIGHEST)
    imag_part = jnp.einsum("pcis,pcjs->cij", rotated, right, precision=lax.Precision.HIGHEST)
    return (real_part, imag_part)


def general_form(samples, taps):
    channels = taps.shape[1]
    tap_count = taps.shape[0]
    inputs_dev = samples.shape[1]
    blocks = samples.reshape(2, inputs_dev, -1, channels)
    frames = blocks.shape[2]
    last_frames = blocks[:, :, frames - (tap_count - 1) :, :]
    history = passed_along(last_frames, "tm", 1)
    filtered = polyphase(blocks, history, taps)
    position = jnp.arange(channels, dtype=jnp.int32)
    spectra = transform(dft_table(position, channels), filtered)
    turned = lax.all_to_all(
        lax.all_to_all(spectra, "grp", split_axis=1, concat_axis=2, tiled=True),
        "tm",
        split_axis=1,
        concat_axis=3,
        tiled=True,
    )
    total = turned.shape[3]
    real_part, imag_part = pair_products(turned, turned)
    return (real_part * (1.0 / total), imag_part * (1.0 / total))


def radix8(values):
    def add(a, b):
        return (a[0] + b[0], a[1] + b[1])

    def sub(a, b):
        return (a[0] - b[0], a[1] - b[1])

    def minus_i(a):
        return (a[1], -a[0])

    def four(x0, x1, x2, x3):
        s, d = add(x0, x2), sub(x0, x2)
        t, e = add(x1, x3), minus_i(sub(x1, x3))
        return add(s, t), add(d, e), sub(s, t), sub(d, e)

    even = four(values[0], values[2], values[4], values[6])
    odd = list(four(values[1], values[3], values[5], values[7]))
    half = math.sqrt(0.5)
    odd[1] = ((odd[1][0] + odd[1][1]) * half, (odd[1][1] - odd[1][0]) * half)
    odd[2] = minus_i(odd[2])
    odd[3] = ((odd[3][1] - odd[3][0]) * half, -(odd[3][0] + odd[3][1]) * half)
    return [add(a, b) for a, b in zip(even, odd)] + [sub(a, b) for a, b in zip(even, odd)]


def split(values):
    high = values.astype(jnp.bfloat16)
    return high, (values - high.astype(jnp.float32)).astype(jnp.bfloat16)


def fused_kernel(
    groups, times, samples_in, taps_in, table_in, twiddle_in, got_ref, *refs
):
    relayed = refs[: len(LATER)]
    (
        frames_ref,
        taps_ref,
        table_ref,
        twiddle_ref,
        early,
        late,
        mixed,
        load_sem,
        halo_sem,
        kept_sem,
        send_sem,
        recv_sem,
        relay_sem,
    ) = refs[len(LATER) :]
    tap_count, channels = taps_ref.shape
    inputs_dev = samples_in.shape[1]
    frames = samples_in.shape[2] // channels
    half, back = frames // 2, tap_count - 1
    devices = groups * times
    near = devices // 2
    share = early.shape[1] // devices
    last = PARTS - 1
    g, t_own = lax.axis_index("grp"), lax.axis_index("tm")
    me = g * times + t_own
    slot = lax.rem(me, near)
    barrier = pltpu.get_barrier_semaphore()

    def place(other):
        return {"grp": other // times, "tm": other % times}

    def paired(step):
        return sum(
            ((me // (1 << b) + step // (1 << b)) % 2) * (1 << b)
            for b in range(devices.bit_length() - 1)
        )

    chunk = 2 * ROWS
    chunks = inputs_dev // chunk
    opening = half - back

    def load(number):
        rows = pl.ds(pl.multiple_of(number * chunk, chunk), chunk)
        return pltpu.make_async_copy(
            samples_in.at[:, rows, pl.ds(opening * channels, (frames - opening) * channels)],
            frames_ref.at[
                :, rows, pl.ds((back + opening) * channels, (frames - opening) * channels)
            ],
            load_sem.at[number],
        )

    load_opening = pltpu.make_async_copy(
        samples_in.at[:, :, pl.ds(0, opening * channels)],
        frames_ref.at[:, :, pl.ds(back * channels, opening * channels)],
        load_sem.at[chunks + 3],
    )

    tables_in = [
        pltpu.make_async_copy(source, target, load_sem.at[chunks + number])
        for number, (source, target) in enumerate(
            ((taps_in, taps_ref), (twiddle_in, twiddle_ref), (table_in, table_ref))
        )
    ]
    tables_in[0].start()
    tables_in[1].start()

    @pl.loop(0, chunks)
    def _(number):
        load(number).start()

    tables_in[2].start()
    load_opening.start()

    @pl.loop(1, devices)
    def _(step):
        pl.semaphore_signal(
            barrier,
            inc=1,
            device_id=place(lax.rem(me + step, devices)),
            device_id_type=pl.DeviceIdType.MESH,
        )

    tables_in[0].wait()
    tables_in[1].wait()

    halo = pltpu.make_async_remote_copy(
        src_ref=samples_in.at[:, :, pl.ds((frames - back) * channels, back * channels)],
        dst_ref=frames_ref.at[:, :, pl.ds(0, back * channels)],
        send_sem=halo_sem.at[0],
        recv_sem=halo_sem.at[1],
        device_id={"grp": g, "tm": lax.rem(t_own + 1, times)},
        device_id_type=pl.DeviceIdType.MESH,
    )

    def filtered(first, loading):
        pairs = half // 2

        @pl.loop(0, pairs * (inputs_dev // ROWS))
        def _(work):
            s = 2 * (work % pairs)
            r = work // pairs
            if loading:
                steps = pairs * (chunk // ROWS)

                @pl.when(work % steps == 0)
                def _():
                    load(work // steps).wait()

            rows = pl.ds(pl.multiple_of(r * ROWS, ROWS), ROWS)
            values = ([], [])
            for n1 in range(RADIX):
                both = ([], [])
                taps = [
                    taps_ref[t : t + 1, n1 * LANES : (n1 + 1) * LANES] for t in range(tap_count)
                ]
                for p in range(2):
                    read = []
                    for t in range(tap_count + 1):
                        start = (s + first + t) * channels + n1 * LANES
                        read.append(
                            frames_ref[p, rows, pl.ds(pl.multiple_of(start, LANES), LANES)]
                        )
                    for f in range(2):
                        acc = taps[0] * read[f]
                        for t in range(1, tap_count):
                            acc = acc + taps[t] * read[f + t]
                        both[f].append(acc)
                for f in range(2):
                    values[f].append(tuple(both[f]))
            for f in range(2):
                put = pl.ds(pl.multiple_of((s + f) * inputs_dev + r * ROWS, ROWS), ROWS)
                for k1, (re, im) in enumerate(radix8(values[f])):
                    if k1:
                        c = twiddle_ref[0, k1 : k1 + 1, :]
                        d = twiddle_ref[1, k1 : k1 + 1, :]
                        re, im = re * c + im * d, im * c - re * d
                    mixed[k1, put, 0:LANES] = re
                    mixed[k1, put, LANES : 2 * LANES] = im

    per_part = RADIX // PARTS
    per_half = ROWS // 2

    def transformed(part, target):
        for inner in range(per_part):
            high, low = split(mixed[part * per_part + inner])
            product = lax.dot_general(
                table_ref[...],
                jnp.concatenate([high, low, high], axis=1),
                (((1,), (1,)), ((), ())),
                preferred_element_type=jnp.float32,
            )
            for p in range(2):
                for pair in range(per_half // 2):
                    start = inner * per_half + p * (per_half // 2) + pair
                    target[part, pl.ds(start, LANES, stride=per_part * per_half), :] = product[
                        p * LANES : (p + 1) * LANES, pair * LANES : (pair + 1) * LANES
                    ]

    def rows_of(source, parts, device):
        first = pl.multiple_of(device * share, share)
        return source.at[pl.ds(parts[0], parts[1] - parts[0]), pl.ds(first, share)]

    def landing(phase, parts):
        return got_ref.at[phase, me, pl.ds(parts[0], parts[1] - parts[0])]

    def far_copy(batch, phase, parts, source, step):
        other = paired(near + step)
        parts = (parts[0], min(parts[1], last))
        return pltpu.make_async_remote_copy(
            src_ref=rows_of(source, parts, other),
            dst_ref=landing(phase, parts),
            send_sem=send_sem.at[batch, near + step],
            recv_sem=recv_sem.at[batch, near + step],
            device_id=place(other),
            device_id_type=pl.DeviceIdType.MESH,
        )

    def near_copy(batch, phase, parts, source, step):
        other = paired(step)
        return pltpu.make_async_remote_copy(
            src_ref=rows_of(source, parts, other),
            dst_ref=landing(phase, parts),
            send_sem=send_sem.at[batch, step],
            recv_sem=recv_sem.at[batch, step],
            device_id=place(other),
            device_id_type=pl.DeviceIdType.MESH,
        )

    def pieces(parts):
        first = 0
        for number, ref in enumerate(relayed if parts[1] == PARTS else ()):
            yield number, ref, first, ref.shape[2]
            first += ref.shape[2]

    def piece_of(source, device, first, count):
        start = pl.multiple_of(device * share + first, ROWS)
        return source.at[last, pl.ds(start, count)]

    def relay_copy(phase, source, step, number, ref, first, count):
        return pltpu.make_async_remote_copy(
            src_ref=piece_of(source, paired(near + step), first, count),
            dst_ref=ref.at[phase, slot],
            send_sem=relay_sem.at[0, phase, number, step],
            recv_sem=relay_sem.at[1, phase, number, step],
            device_id=place(paired(step)),
            device_id_type=pl.DeviceIdType.MESH,
        )

    def kept(batch, phase, parts, source):
        yield pltpu.make_async_copy(
            rows_of(source, parts, me), landing(phase, parts), kept_sem.at[batch]
        )
        for number, ref, first, count in pieces(parts):
            yield pltpu.make_async_copy(
                piece_of(source, paired(near), first, count),
                ref.at[phase, slot],
                relay_sem.at[0, phase, number, 0],
            )

    def each_copy(batch, phase, parts, source, act):
        @pl.loop(0, near)
        def _(step):
            if parts[0] < last:
                act(far_copy(batch, phase, parts, source, step))

            @pl.when(step > 0)
            def _():
                act(near_copy(batch, phase, parts, source, step))
                for args in pieces(parts):
                    act(relay_copy(phase, source, step, *args))

        for copy in kept(batch, phase, parts, source):
            act(copy)

    batches = [
        (0, 0, (0, 1), early),
        (1, 0, (1, PARTS), early),
        (2, 1, (0, PARTS), late),
    ]

    filtered(half, True)
    tables_in[2].wait()
    transformed(0, early)
    pl.semaphore_wait(barrier, devices - 1)

    @pl.when(t_own < times - 1)
    def _():
        halo.start()

    each_copy(*batches[0], lambda copy: copy.start())
    for part in range(1, PARTS):
        transformed(part, early)
    each_copy(*batches[1], lambda copy: copy.start())

    @pl.when(t_own == 0)
    def _():
        frames_ref[:, :, 0 : back * channels] = jnp.zeros(
            (2, inputs_dev, back * channels), jnp.float32
        )

    @pl.when(t_own > 0)
    def _():
        halo.wait_recv()

    load_opening.wait()
    filtered(0, False)
    for part in range(PARTS):
        transformed(part, late)
    each_copy(*batches[2], lambda copy: copy.start())

    @pl.when(t_own < times - 1)
    def _():
        halo.wait_send()

    for batch in batches:
        each_copy(*batch, lambda copy: copy.wait())


def tables(channels):
    n2 = np.arange(LANES)
    phase = 2.0 * np.pi * np.outer(n2, n2) / LANES
    c, s = np.cos(phase), np.sin(phase)
    table = (np.block([[c, s], [-s, c]]) / math.sqrt(channels)).astype(np.float32)
    high = table.astype(jnp.bfloat16)
    low = (table - high.astype(np.float32)).astype(jnp.bfloat16)
    turn = 2.0 * np.pi * np.outer(np.arange(RADIX), n2) / channels
    twiddle = np.stack([np.cos(turn), np.sin(turn)])
    return jnp.asarray(np.concatenate([high, high, low], axis=1)), jnp.asarray(twiddle, jnp.float32)


def make_spectra(samples, taps, groups, times):
    tap_count, channels = taps.shape
    inputs_dev = samples.shape[1]
    frames = samples.shape[2] // channels
    half = frames // 2
    devices = groups * times
    table, twiddle = tables(channels)
    rows = channels * ROWS // 2 // PARTS

    def body(*refs):
        fused_kernel(groups, times, *refs)

    return pl.pallas_call(
        body,
        out_shape=[
            jax.ShapeDtypeStruct((2, devices, PARTS, rows // devices, LANES), jnp.float32)
        ]
        + [
            jax.ShapeDtypeStruct((2, devices // 2, count * ROWS // 2, LANES), jnp.float32)
            for count in LATER
        ],
        in_specs=[pl.BlockSpec(memory_space=pltpu.HBM)] * 4,
        out_specs=[pl.BlockSpec(memory_space=pltpu.VMEM)] * (1 + len(LATER)),
        scratch_shapes=[
            pltpu.VMEM((2, inputs_dev, (frames + tap_count - 1) * channels), jnp.float32),
            pltpu.VMEM(taps.shape, jnp.float32),
            pltpu.VMEM(table.shape, jnp.bfloat16),
            pltpu.VMEM(twiddle.shape, jnp.float32),
            pltpu.VMEM((PARTS, rows, LANES), jnp.float32),
            pltpu.VMEM((PARTS, rows, LANES), jnp.float32),
            pltpu.VMEM((RADIX, half * inputs_dev, 2 * LANES), jnp.float32),
            pltpu.SemaphoreType.DMA((inputs_dev // (2 * ROWS) + 4,)),
            pltpu.SemaphoreType.DMA((2,)),
            pltpu.SemaphoreType.DMA((3,)),
            pltpu.SemaphoreType.DMA((3, devices)),
            pltpu.SemaphoreType.DMA((3, devices)),
            pltpu.SemaphoreType.DMA((2, 2, len(LATER), devices // 2)),
        ],
        compiler_params=pltpu.CompilerParams(
            collective_id=0, has_side_effects=True, vmem_limit_bytes=40 * MIB
        ),
    )(*(pltpu.with_memory_space_constraint(x, pltpu.HBM) for x in (samples, taps, table, twiddle)))


def gram_kernel(groups, times, total, start, count, relayed, got_ref, *refs):
    real_out, imag_out, real_ref, imag_ref, sem = refs[-5:]
    near = groups * times // 2
    own_channels = real_out.shape[0]
    in_first = lax.axis_index("grp") < groups // 2 if relayed else None
    lane = lax.broadcasted_iota(jnp.int32, (ROWS, LANES), 1)
    row = lax.broadcasted_iota(jnp.int32, (ROWS, LANES), 0)
    low, upper = lane < LANES // 2, row < ROWS // 2
    first = row % (ROWS // 2) < ROWS // 4

    def stacked(values):
        high, low_part = split(values)
        return jnp.concatenate([high, low_part, low_part, high], axis=0)

    def channel_of(pair):
        per_block = RADIX // PARTS // 2
        blocks = own_channels // RADIX
        block = pair // per_block
        return (
            (block % blocks) * RADIX + (block // blocks) * (2 * per_block) + 2 * (pair % per_block)
        )

    def writes(turn, channel):
        at = turn % SLOTS
        return [
            pltpu.make_async_copy(ref.at[at], out.at[channel], sem.at[number, at])
            for number, (ref, out) in enumerate(((real_ref, real_out), (imag_ref, imag_out)))
        ]

    @pl.loop(0, count // 2)
    def _(step):
        pair = start // 2 + step
        for parity in range(2):
            def tile(source):
                a, b = got_ref[0, source, pair], got_ref[1, source, pair]
                if relayed:
                    is_near = in_first if source < near else jnp.logical_not(in_first)
                    a = jnp.where(is_near, a, refs[0][0, source % near, step])
                    b = jnp.where(is_near, b, refs[0][1, source % near, step])
                if parity == 0:
                    return jnp.where(upper, a, pltpu.roll(b, ROWS // 2, 0))
                return jnp.where(upper, pltpu.roll(a, ROWS // 2, 0), b)

            plain, turned = [], []
            for t in range(times):
                parts = ([], [])
                for m in range(groups // 2):
                    x, y = tile(2 * m * times + t), tile((2 * m + 1) * times + t)
                    parts[0].append(jnp.where(low, x, pltpu.roll(y, LANES // 2, 1)))
                    parts[1].append(jnp.where(low, pltpu.roll(x, LANES // 2, 1), y))
                for tiles in parts:
                    plain.append(jnp.concatenate(tiles, axis=1))
                    turned.append(
                        jnp.concatenate(
                            [
                                jnp.where(
                                    first,
                                    -pltpu.roll(v, ROWS - ROWS // 4, 0),
                                    pltpu.roll(v, ROWS // 4, 0),
                                )
                                for v in tiles
                            ],
                            axis=1,
                        )
                    )

            whole = jnp.concatenate(plain, axis=0)
            high, low_part = split(whole * (1.0 / total))
            left = jnp.concatenate(
                [high.astype(jnp.float32), low_part.astype(jnp.float32)], axis=0
            ).T.astype(jnp.bfloat16)
            left = jnp.concatenate([left, left], axis=1)
            turn = 2 * step + parity
            at = turn % SLOTS

            @pl.when(turn >= SLOTS)
            def _():
                for write in writes(turn, 0):
                    write.wait()

            real_ref[at] = jnp.dot(left, stacked(whole), preferred_element_type=jnp.float32)
            imag_ref[at] = jnp.dot(
                left,
                stacked(jnp.concatenate(turned, axis=0)),
                preferred_element_type=jnp.float32,
            )
            for write in writes(turn, channel_of(pair) + parity):
                write.start()

    for turn in range(max(0, count - SLOTS), count):
        for write in writes(turn, 0):
            write.wait()


def gram(got, groups, times, total, inputs, start, count, arrived=None, so_far=()):
    own_channels = 2 * got.shape[2]
    relayed = arrived is not None

    def body(*refs):
        gram_kernel(groups, times, total, start, count, relayed, *refs)

    shape = jax.ShapeDtypeStruct((own_channels, inputs, inputs), jnp.float32)
    here = 1 + relayed
    return pl.pallas_call(
        body,
        out_shape=(shape, shape),
        in_specs=[pl.BlockSpec(memory_space=pltpu.VMEM)] * here
        + [pl.BlockSpec(memory_space=pl.ANY)] * len(so_far),
        out_specs=(pl.BlockSpec(memory_space=pltpu.HBM),) * 2,
        input_output_aliases={here + i: i for i in range(len(so_far))},
        scratch_shapes=[
            pltpu.VMEM((SLOTS, inputs, inputs), jnp.float32),
            pltpu.VMEM((SLOTS, inputs, inputs), jnp.float32),
            pltpu.SemaphoreType.DMA((2, SLOTS)),
        ],
        cost_estimate=pl.CostEstimate(
            flops=count * 2 * inputs * inputs * 4 * ROWS * times * 4,
            bytes_accessed=count * 2 * inputs * inputs * 4,
            transcendentals=0,
        ),
        compiler_params=pltpu.CompilerParams(vmem_limit_bytes=24 * MIB),
    )(got, *((arrived,) if relayed else ()), *so_far)


def solution(mesh):
    groups, times = mesh.shape["grp"], mesh.shape["tm"]
    devices = groups * times

    def per_device(samples, taps):
        tap_count, channels = taps.shape
        inputs_dev = samples.shape[1]
        frames = samples.shape[2] // channels
        tiled = (
            channels == RADIX * LANES
            and inputs_dev * 2 == LANES
            and frames == ROWS
            and groups % 2 == 0
            and channels % (RADIX * devices) == 0
            and channels // devices // PARTS == sum(LATER)
            and devices & (devices - 1) == 0
            and tap_count - 1 <= frames // 2
            and 2 * frames * times * 2 == LANES
        )
        if not tiled:
            return general_form(samples, taps)
        got, *relayed = make_spectra(samples, taps, groups, times)
        own = channels // devices
        across = [(g, (g + groups // 2) % groups) for g in range(groups)]
        got = got.reshape(2, devices, own // 2, ROWS, LANES)
        sizes = (groups, times, frames * times, inputs_dev * groups)
        bounds = (0,) + AHEAD + (own - sum(LATER),)
        arrived, so_far = [], ()
        for number, part in enumerate(relayed):
            if number:
                part, so_far = lax.optimization_barrier((part, so_far))
            arrived.append(lax.ppermute(part, "grp", across))
            start, end = bounds[number], bounds[number + 1]
            so_far = gram(got, *sizes, start, end - start, None, so_far)
        start = bounds[-1]
        for count, part in zip(LATER, arrived):
            part = part.reshape(2, devices // 2, count // 2, ROWS, LANES)
            so_far = gram(got, *sizes, start, count, part, so_far)
            start += count
        return so_far

    return jax.shard_map(
        per_device,
        mesh=mesh,
        in_specs=(P(None, "grp", "tm"), P()),
        out_specs=(P(("grp", "tm"), None, None), P(("grp", "tm"), None, None)),
        check_vma=False,
    )
```

```python
import math

import numpy as np
import jax
import jax.numpy as jnp
from jax import lax
from jax.experimental import pallas as pl
from jax.experimental.pallas import tpu as pltpu
from jax.sharding import PartitionSpec as P

RADIX = 8
LANES = 128
ROWS = 8
MIB = 1 << 20
PARTS = 4
SLOTS = 4
LATER = (4, 4)
AHEAD = (4,)


def passed_along(value, axis, steps):
    count = lax.axis_size(axis)
    leading, last = (max(0, -steps), min(count, count - steps))
    return lax.ppermute(value, axis, [(source, source + steps) for source in range(leading, last)])


def dft_table(order, channels):
    index = jnp.arange(channels, dtype=jnp.int32)
    phase = (order[:, None] * index[None, :] % channels).astype(jnp.float32) * (
        2.0 * math.pi / channels
    )
    factor = 1.0 / math.sqrt(channels)
    cosine = jnp.cos(phase) * factor
    sine = jnp.sin(phase) * factor
    upper = jnp.concatenate([cosine, sine], axis=1)
    lower = jnp.concatenate([-sine, cosine], axis=1)
    return jnp.concatenate([upper, lower], axis=0)


def polyphase(blocks, history, taps):
    extended = jnp.concatenate([history, blocks], axis=2)
    frames = blocks.shape[2]
    filtered = jnp.zeros(blocks.shape, jnp.float32)
    for tap in range(taps.shape[0]):
        filtered = filtered + taps[tap][None, None, None, :] * extended[:, :, tap : tap + frames, :]
    return filtered


def transform(table, filtered):
    channels = filtered.shape[3]
    product = lax.dot_general(
        table.reshape(2 * channels, 2, channels),
        filtered,
        (((1, 2), (0, 3)), ((), ())),
        precision=lax.Precision.HIGHEST,
    )
    return product.reshape(2, channels, filtered.shape[1], filtered.shape[2])


def pair_products(left, right):
    rotated = jnp.stack([left[1], -left[0]])
    real_part = jnp.einsum("pcis,pcjs->cij", left, right, precision=lax.Precision.HIGHEST)
    imag_part = jnp.einsum("pcis,pcjs->cij", rotated, right, precision=lax.Precision.HIGHEST)
    return (real_part, imag_part)


def general_form(samples, taps):
    channels = taps.shape[1]
    tap_count = taps.shape[0]
    inputs_dev = samples.shape[1]
    blocks = samples.reshape(2, inputs_dev, -1, channels)
    frames = blocks.shape[2]
    last_frames = blocks[:, :, frames - (tap_count - 1) :, :]
    history = passed_along(last_frames, "tm", 1)
    filtered = polyphase(blocks, history, taps)
    position = jnp.arange(channels, dtype=jnp.int32)
    spectra = transform(dft_table(position, channels), filtered)
    turned = lax.all_to_all(
        lax.all_to_all(spectra, "grp", split_axis=1, concat_axis=2, tiled=True),
        "tm",
        split_axis=1,
        concat_axis=3,
        tiled=True,
    )
    total = turned.shape[3]
    real_part, imag_part = pair_products(turned, turned)
    return (real_part * (1.0 / total), imag_part * (1.0 / total))


def radix8(values):
    def add(a, b):
        return (a[0] + b[0], a[1] + b[1])

    def sub(a, b):
        return (a[0] - b[0], a[1] - b[1])

    def minus_i(a):
        return (a[1], -a[0])

    def four(x0, x1, x2, x3):
        s, d = add(x0, x2), sub(x0, x2)
        t, e = add(x1, x3), minus_i(sub(x1, x3))
        return add(s, t), add(d, e), sub(s, t), sub(d, e)

    even = four(values[0], values[2], values[4], values[6])
    odd = list(four(values[1], values[3], values[5], values[7]))
    half = math.sqrt(0.5)
    odd[1] = ((odd[1][0] + odd[1][1]) * half, (odd[1][1] - odd[1][0]) * half)
    odd[2] = minus_i(odd[2])
    odd[3] = ((odd[3][1] - odd[3][0]) * half, -(odd[3][0] + odd[3][1]) * half)
    return [add(a, b) for a, b in zip(even, odd)] + [sub(a, b) for a, b in zip(even, odd)]


def split(values):
    high = values.astype(jnp.bfloat16)
    return high, (values - high.astype(jnp.float32)).astype(jnp.bfloat16)


def fused_kernel(
    groups, times, samples_in, taps_in, table_in, twiddle_in, got_ref, *refs
):
    relayed = refs[: len(LATER)]
    (
        frames_ref,
        taps_ref,
        table_ref,
        twiddle_ref,
        early,
        late,
        mixed,
        load_sem,
        halo_sem,
        kept_sem,
        send_sem,
        recv_sem,
        relay_sem,
    ) = refs[len(LATER) :]
    tap_count, channels = taps_ref.shape
    inputs_dev = samples_in.shape[1]
    frames = samples_in.shape[2] // channels
    half, back = frames // 2, tap_count - 1
    devices = groups * times
    near = devices // 2
    share = early.shape[1] // devices
    last = PARTS - 1
    g, t_own = lax.axis_index("grp"), lax.axis_index("tm")
    me = g * times + t_own
    slot = lax.rem(me, near)
    barrier = pltpu.get_barrier_semaphore()

    def place(other):
        return {"grp": other // times, "tm": other % times}

    def paired(step):
        return sum(
            ((me // (1 << b) + step // (1 << b)) % 2) * (1 << b)
            for b in range(devices.bit_length() - 1)
        )

    chunk = 2 * ROWS
    chunks = inputs_dev // chunk
    opening = half - back

    def load(number):
        rows = pl.ds(pl.multiple_of(number * chunk, chunk), chunk)
        return pltpu.make_async_copy(
            samples_in.at[:, rows, pl.ds(opening * channels, (frames - opening) * channels)],
            frames_ref.at[
                :, rows, pl.ds((back + opening) * channels, (frames - opening) * channels)
            ],
            load_sem.at[number],
        )

    load_opening = pltpu.make_async_copy(
        samples_in.at[:, :, pl.ds(0, opening * channels)],
        frames_ref.at[:, :, pl.ds(back * channels, opening * channels)],
        load_sem.at[chunks + 3],
    )

    tables_in = [
        pltpu.make_async_copy(source, target, load_sem.at[chunks + number])
        for number, (source, target) in enumerate(
            ((taps_in, taps_ref), (twiddle_in, twiddle_ref), (table_in, table_ref))
        )
    ]
    tables_in[0].start()
    tables_in[1].start()

    @pl.loop(0, chunks)
    def _(number):
        load(number).start()

    tables_in[2].start()
    load_opening.start()

    @pl.loop(1, devices)
    def _(step):
        pl.semaphore_signal(
            barrier,
            inc=1,
            device_id=place(lax.rem(me + step, devices)),
            device_id_type=pl.DeviceIdType.MESH,
        )

    tables_in[0].wait()
    tables_in[1].wait()

    halo = pltpu.make_async_remote_copy(
        src_ref=samples_in.at[:, :, pl.ds((frames - back) * channels, back * channels)],
        dst_ref=frames_ref.at[:, :, pl.ds(0, back * channels)],
        send_sem=halo_sem.at[0],
        recv_sem=halo_sem.at[1],
        device_id={"grp": g, "tm": lax.rem(t_own + 1, times)},
        device_id_type=pl.DeviceIdType.MESH,
    )

    def filtered(first, loading):
        pairs = half // 2

        @pl.loop(0, pairs * (inputs_dev // ROWS))
        def _(work):
            s = 2 * (work % pairs)
            r = work // pairs
            if loading:
                steps = pairs * (chunk // ROWS)

                @pl.when(work % steps == 0)
                def _():
                    load(work // steps).wait()

            rows = pl.ds(pl.multiple_of(r * ROWS, ROWS), ROWS)
            values = ([], [])
            for n1 in range(RADIX):
                both = ([], [])
                taps = [
                    taps_ref[t : t + 1, n1 * LANES : (n1 + 1) * LANES] for t in range(tap_count)
                ]
                for p in range(2):
                    read = []
                    for t in range(tap_count + 1):
                        start = (s + first + t) * channels + n1 * LANES
                        read.append(
                            frames_ref[p, rows, pl.ds(pl.multiple_of(start, LANES), LANES)]
                        )
                    for f in range(2):
                        acc = taps[0] * read[f]
                        for t in range(1, tap_count):
                            acc = acc + taps[t] * read[f + t]
                        both[f].append(acc)
                for f in range(2):
                    values[f].append(tuple(both[f]))
            for f in range(2):
                put = pl.ds(pl.multiple_of((s + f) * inputs_dev + r * ROWS, ROWS), ROWS)
                for k1, (re, im) in enumerate(radix8(values[f])):
                    if k1:
                        c = twiddle_ref[0, k1 : k1 + 1, :]
                        d = twiddle_ref[1, k1 : k1 + 1, :]
                        re, im = re * c + im * d, im * c - re * d
                    mixed[k1, put, 0:LANES] = re
                    mixed[k1, put, LANES : 2 * LANES] = im

    per_part = RADIX // PARTS
    per_half = ROWS // 2

    def transformed(part, target):
        for inner in range(per_part):
            high, low = split(mixed[part * per_part + inner])
            product = lax.dot_general(
                table_ref[...],
                jnp.concatenate([high, low, high], axis=1),
                (((1,), (1,)), ((), ())),
                preferred_element_type=jnp.float32,
            )
            for p in range(2):
                for pair in range(per_half // 2):
                    start = inner * per_half + p * (per_half // 2) + pair
                    target[part, pl.ds(start, LANES, stride=per_part * per_half), :] = product[
                        p * LANES : (p + 1) * LANES, pair * LANES : (pair + 1) * LANES
                    ]

    def rows_of(source, parts, device):
        first = pl.multiple_of(device * share, share)
        return source.at[pl.ds(parts[0], parts[1] - parts[0]), pl.ds(first, share)]

    def landing(phase, parts):
        return got_ref.at[phase, me, pl.ds(parts[0], parts[1] - parts[0])]

    def far_copy(batch, phase, parts, source, step):
        other = paired(near + step)
        parts = (parts[0], min(parts[1], last))
        return pltpu.make_async_remote_copy(
            src_ref=rows_of(source, parts, other),
            dst_ref=landing(phase, parts),
            send_sem=send_sem.at[batch, near + step],
            recv_sem=recv_sem.at[batch, near + step],
            device_id=place(other),
            device_id_type=pl.DeviceIdType.MESH,
        )

    def near_copy(batch, phase, parts, source, step):
        other = paired(step)
        return pltpu.make_async_remote_copy(
            src_ref=rows_of(source, parts, other),
            dst_ref=landing(phase, parts),
            send_sem=send_sem.at[batch, step],
            recv_sem=recv_sem.at[batch, step],
            device_id=place(other),
            device_id_type=pl.DeviceIdType.MESH,
        )

    def pieces(parts):
        first = 0
        for number, ref in enumerate(relayed if parts[1] == PARTS else ()):
            yield number, ref, first, ref.shape[2]
            first += ref.shape[2]

    def piece_of(source, device, first, count):
        start = pl.multiple_of(device * share + first, ROWS)
        return source.at[last, pl.ds(start, count)]

    def relay_copy(phase, source, step, number, ref, first, count):
        return pltpu.make_async_remote_copy(
            src_ref=piece_of(source, paired(near + step), first, count),
            dst_ref=ref.at[phase, slot],
            send_sem=relay_sem.at[0, phase, number, step],
            recv_sem=relay_sem.at[1, phase, number, step],
            device_id=place(paired(step)),
            device_id_type=pl.DeviceIdType.MESH,
        )

    def kept(batch, phase, parts, source):
        yield pltpu.make_async_copy(
            rows_of(source, parts, me), landing(phase, parts), kept_sem.at[batch]
        )
        for number, ref, first, count in pieces(parts):
            yield pltpu.make_async_copy(
                piece_of(source, paired(near), first, count),
                ref.at[phase, slot],
                relay_sem.at[0, phase, number, 0],
            )

    def each_copy(batch, phase, far_parts, near_parts, source, act):
        @pl.loop(0, near)
        def _(step):
            act(far_copy(batch, phase, far_parts, source, step))
            if near_parts:

                @pl.when(step > 0)
                def _():
                    act(near_copy(batch, phase, near_parts, source, step))
                    for args in pieces(near_parts):
                        act(relay_copy(phase, source, step, *args))

        if near_parts:
            for copy in kept(batch, phase, near_parts, source):
                act(copy)

    batches = [
        (0, 0, (0, 1), None, early),
        (1, 0, (1, PARTS), (0, PARTS), early),
        (2, 1, (0, PARTS), (0, PARTS), late),
    ]

    filtered(half, True)
    tables_in[2].wait()
    transformed(0, early)
    pl.semaphore_wait(barrier, devices - 1)

    @pl.when(t_own < times - 1)
    def _():
        halo.start()

    each_copy(*batches[0], lambda copy: copy.start())
    for part in range(1, PARTS):
        transformed(part, early)
    each_copy(*batches[1], lambda copy: copy.start())

    @pl.when(t_own == 0)
    def _():
        frames_ref[:, :, 0 : back * channels] = jnp.zeros(
            (2, inputs_dev, back * channels), jnp.float32
        )

    @pl.when(t_own > 0)
    def _():
        halo.wait_recv()

    load_opening.wait()
    filtered(0, False)
    for part in range(PARTS):
        transformed(part, late)
    each_copy(*batches[2], lambda copy: copy.start())

    @pl.when(t_own < times - 1)
    def _():
        halo.wait_send()

    for batch in batches:
        each_copy(*batch, lambda copy: copy.wait())


def tables(channels):
    n2 = np.arange(LANES)
    phase = 2.0 * np.pi * np.outer(n2, n2) / LANES
    c, s = np.cos(phase), np.sin(phase)
    table = (np.block([[c, s], [-s, c]]) / math.sqrt(channels)).astype(np.float32)
    high = table.astype(jnp.bfloat16)
    low = (table - high.astype(np.float32)).astype(jnp.bfloat16)
    turn = 2.0 * np.pi * np.outer(np.arange(RADIX), n2) / channels
    twiddle = np.stack([np.cos(turn), np.sin(turn)])
    return jnp.asarray(np.concatenate([high, high, low], axis=1)), jnp.asarray(twiddle, jnp.float32)


def make_spectra(samples, taps, groups, times):
    tap_count, channels = taps.shape
    inputs_dev = samples.shape[1]
    frames = samples.shape[2] // channels
    half = frames // 2
    devices = groups * times
    table, twiddle = tables(channels)
    rows = channels * ROWS // 2 // PARTS

    def body(*refs):
        fused_kernel(groups, times, *refs)

    return pl.pallas_call(
        body,
        out_shape=[
            jax.ShapeDtypeStruct((2, devices, PARTS, rows // devices, LANES), jnp.float32)
        ]
        + [
            jax.ShapeDtypeStruct((2, devices // 2, count * ROWS // 2, LANES), jnp.float32)
            for count in LATER
        ],
        in_specs=[pl.BlockSpec(memory_space=pltpu.HBM)] * 4,
        out_specs=[pl.BlockSpec(memory_space=pltpu.VMEM)] * (1 + len(LATER)),
        scratch_shapes=[
            pltpu.VMEM((2, inputs_dev, (frames + tap_count - 1) * channels), jnp.float32),
            pltpu.VMEM(taps.shape, jnp.float32),
            pltpu.VMEM(table.shape, jnp.bfloat16),
            pltpu.VMEM(twiddle.shape, jnp.float32),
            pltpu.VMEM((PARTS, rows, LANES), jnp.float32),
            pltpu.VMEM((PARTS, rows, LANES), jnp.float32),
            pltpu.VMEM((RADIX, half * inputs_dev, 2 * LANES), jnp.float32),
            pltpu.SemaphoreType.DMA((inputs_dev // (2 * ROWS) + 4,)),
            pltpu.SemaphoreType.DMA((2,)),
            pltpu.SemaphoreType.DMA((3,)),
            pltpu.SemaphoreType.DMA((3, devices)),
            pltpu.SemaphoreType.DMA((3, devices)),
            pltpu.SemaphoreType.DMA((2, 2, len(LATER), devices // 2)),
        ],
        compiler_params=pltpu.CompilerParams(
            collective_id=0, has_side_effects=True, vmem_limit_bytes=40 * MIB
        ),
    )(*(pltpu.with_memory_space_constraint(x, pltpu.HBM) for x in (samples, taps, table, twiddle)))


def gram_kernel(groups, times, total, start, count, relayed, got_ref, *refs):
    real_out, imag_out, real_ref, imag_ref, sem = refs[-5:]
    near = groups * times // 2
    own_channels = real_out.shape[0]
    in_first = lax.axis_index("grp") < groups // 2 if relayed else None
    lane = lax.broadcasted_iota(jnp.int32, (ROWS, LANES), 1)
    row = lax.broadcasted_iota(jnp.int32, (ROWS, LANES), 0)
    low, upper = lane < LANES // 2, row < ROWS // 2
    first = row % (ROWS // 2) < ROWS // 4

    def stacked(values):
        high, low_part = split(values)
        return jnp.concatenate([high, low_part, low_part, high], axis=0)

    def channel_of(pair):
        per_block = RADIX // PARTS // 2
        blocks = own_channels // RADIX
        block = pair // per_block
        return (
            (block % blocks) * RADIX + (block // blocks) * (2 * per_block) + 2 * (pair % per_block)
        )

    def writes(turn, channel):
        at = turn % SLOTS
        return [
            pltpu.make_async_copy(ref.at[at], out.at[channel], sem.at[number, at])
            for number, (ref, out) in enumerate(((real_ref, real_out), (imag_ref, imag_out)))
        ]

    @pl.loop(0, count // 2)
    def _(step):
        pair = start // 2 + step
        for parity in range(2):
            def tile(source):
                a, b = got_ref[0, source, pair], got_ref[1, source, pair]
                if relayed:
                    is_near = in_first if source < near else jnp.logical_not(in_first)
                    a = jnp.where(is_near, a, refs[0][0, source % near, step])
                    b = jnp.where(is_near, b, refs[0][1, source % near, step])
                if parity == 0:
                    return jnp.where(upper, a, pltpu.roll(b, ROWS // 2, 0))
                return jnp.where(upper, pltpu.roll(a, ROWS // 2, 0), b)

            plain, turned = [], []
            for t in range(times):
                parts = ([], [])
                for m in range(groups // 2):
                    x, y = tile(2 * m * times + t), tile((2 * m + 1) * times + t)
                    parts[0].append(jnp.where(low, x, pltpu.roll(y, LANES // 2, 1)))
                    parts[1].append(jnp.where(low, pltpu.roll(x, LANES // 2, 1), y))
                for tiles in parts:
                    plain.append(jnp.concatenate(tiles, axis=1))
                    turned.append(
                        jnp.concatenate(
                            [
                                jnp.where(
                                    first,
                                    -pltpu.roll(v, ROWS - ROWS // 4, 0),
                                    pltpu.roll(v, ROWS // 4, 0),
                                )
                                for v in tiles
                            ],
                            axis=1,
                        )
                    )

            whole = jnp.concatenate(plain, axis=0)
            high, low_part = split(whole * (1.0 / total))
            left = jnp.concatenate(
                [high.astype(jnp.float32), low_part.astype(jnp.float32)], axis=0
            ).T.astype(jnp.bfloat16)
            left = jnp.concatenate([left, left], axis=1)
            turn = 2 * step + parity
            at = turn % SLOTS

            @pl.when(turn >= SLOTS)
            def _():
                for write in writes(turn, 0):
                    write.wait()

            real_ref[at] = jnp.dot(left, stacked(whole), preferred_element_type=jnp.float32)
            imag_ref[at] = jnp.dot(
                left,
                stacked(jnp.concatenate(turned, axis=0)),
                preferred_element_type=jnp.float32,
            )
            for write in writes(turn, channel_of(pair) + parity):
                write.start()

    for turn in range(max(0, count - SLOTS), count):
        for write in writes(turn, 0):
            write.wait()


def gram(got, groups, times, total, inputs, start, count, arrived=None, so_far=()):
    own_channels = 2 * got.shape[2]
    relayed = arrived is not None

    def body(*refs):
        gram_kernel(groups, times, total, start, count, relayed, *refs)

    shape = jax.ShapeDtypeStruct((own_channels, inputs, inputs), jnp.float32)
    here = 1 + relayed
    return pl.pallas_call(
        body,
        out_shape=(shape, shape),
        in_specs=[pl.BlockSpec(memory_space=pltpu.VMEM)] * here
        + [pl.BlockSpec(memory_space=pl.ANY)] * len(so_far),
        out_specs=(pl.BlockSpec(memory_space=pltpu.HBM),) * 2,
        input_output_aliases={here + i: i for i in range(len(so_far))},
        scratch_shapes=[
            pltpu.VMEM((SLOTS, inputs, inputs), jnp.float32),
            pltpu.VMEM((SLOTS, inputs, inputs), jnp.float32),
            pltpu.SemaphoreType.DMA((2, SLOTS)),
        ],
        cost_estimate=pl.CostEstimate(
            flops=count * 2 * inputs * inputs * 4 * ROWS * times * 4,
            bytes_accessed=count * 2 * inputs * inputs * 4,
            transcendentals=0,
        ),
        compiler_params=pltpu.CompilerParams(vmem_limit_bytes=24 * MIB),
    )(got, *((arrived,) if relayed else ()), *so_far)


def solution(mesh):
    groups, times = mesh.shape["grp"], mesh.shape["tm"]
    devices = groups * times

    def per_device(samples, taps):
        tap_count, channels = taps.shape
        inputs_dev = samples.shape[1]
        frames = samples.shape[2] // channels
        tiled = (
            channels == RADIX * LANES
            and inputs_dev * 2 == LANES
            and frames == ROWS
            and groups % 2 == 0
            and channels % (RADIX * devices) == 0
            and channels // devices // PARTS == sum(LATER)
            and devices & (devices - 1) == 0
            and tap_count - 1 <= frames // 2
            and 2 * frames * times * 2 == LANES
        )
        if not tiled:
            return general_form(samples, taps)
        got, *relayed = make_spectra(samples, taps, groups, times)
        own = channels // devices
        across = [(g, (g + groups // 2) % groups) for g in range(groups)]
        got = got.reshape(2, devices, own // 2, ROWS, LANES)
        sizes = (groups, times, frames * times, inputs_dev * groups)
        bounds = (0,) + AHEAD + (own - sum(LATER),)
        arrived, so_far = [], ()
        for number, part in enumerate(relayed):
            if number:
                part, so_far = lax.optimization_barrier((part, so_far))
            arrived.append(lax.ppermute(part, "grp", across))
            start, end = bounds[number], bounds[number + 1]
            so_far = gram(got, *sizes, start, end - start, None, so_far)
        start = bounds[-1]
        for count, part in zip(LATER, arrived):
            part = part.reshape(2, devices // 2, count // 2, ROWS, LANES)
            so_far = gram(got, *sizes, start, count, part, so_far)
            start += count
        return so_far

    return jax.shard_map(
        per_device,
        mesh=mesh,
        in_specs=(P(None, "grp", "tm"), P()),
        out_specs=(P(("grp", "tm"), None, None), P(("grp", "tm"), None, None)),
        check_vma=False,
    )
```
